32 devices in a mesh: dp: 16 (over z, x, core), mp: 2 (over y).
Axes of the slice: x: 2, y: 2, z: 4, core: 2. Of those that a mesh axis runs over, the one named last changes fastest.
Arguments:
- layer_input: bfloat16 [2, 24576, 1152], P(None, 'dp', 'mp'), may hold values from -6 to 6
- skip_input: bfloat16 [2, 24576, 1152], P(None, 'dp', 'mp'), may hold values from -6 to 6
- segments: int32 [2, 24576], P(None, 'dp'), may hold values from 0 to 5, as said below
- skip_weight: bfloat16 [2, 1152, 1152], P(None, 'mp'), may hold values from -0.125 to 0.125
- skip_bias: bfloat16 [1152], replicated, may hold values from -1.796875 to 1.796875
- attn_norm_gain: bfloat16 [1152], replicated, may hold values from 0.25 to 1.75
- attn_norm_bias: bfloat16 [1152], replicated, may hold values from -1.796875 to 1.796875
- qkv_weight: bfloat16 [1152, 3, 1152], P(None, None, 'mp'), may hold values from -0.25 to 0.25
- proj_weight: bfloat16 [1152, 1152], P('mp'), may hold values from -0.375 to 0.375
- proj_bias: bfloat16 [1152], replicated, may hold values from -1.796875 to 1.796875
- mlp_norm_gain: bfloat16 [1152], replicated, may hold values from 0.25 to 1.75
- mlp_norm_bias: bfloat16 [1152], replicated, may hold values from -1.796875 to 1.796875
- up_weight: bfloat16 [1152, 4608], P(None, 'mp'), may hold values from -0.1875 to 0.1875
- up_bias: bfloat16 [4608], P('mp'), may hold values from -3 to 3
- down_weight: bfloat16 [4608, 1152], P('mp'), may hold values from -0.125 to 0.125
- down_bias: bfloat16 [1152], replicated, may hold values from -1.796875 to 1.796875
- cotangent: bfloat16 [2, 24576, 1152], P(None, ('dp', 'mp')), may hold values from -6 to 6
Outputs:
- layer_output: bfloat16 [2, 24576, 1152], P(None, ('dp', 'mp'))
- input_grad: bfloat16 [2, 24576, 1152], P(None, 'dp', 'mp')
- skip_input_grad: bfloat16 [2, 24576, 1152], P(None, 'dp', 'mp')
- skip_weight_grad: float32 [2, 1152, 1152], P(None, 'mp', 'dp')
- skip_bias_grad: float32 [1152], replicated
- attn_norm_gain_grad: float32 [1152], replicated
- attn_norm_bias_grad: float32 [1152], replicated
- qkv_weight_grad: float32 [1152, 3, 1152], P('dp', None, 'mp')
- proj_weight_grad: float32 [1152, 1152], P('mp', 'dp')
- proj_bias_grad: float32 [1152], replicated
- mlp_norm_gain_grad: float32 [1152], replicated
- mlp_norm_bias_grad: float32 [1152], replicated
- up_weight_grad: float32 [1152, 4608], P('dp', 'mp')
- up_bias_grad: float32 [4608], replicated
- down_weight_grad: float32 [4608, 1152], P('mp', 'dp')
- down_bias_grad: float32 [1152], replicated
The draws below stay inside these ranges and needn't reach their ends.
Inputs may be any that keep to these rules, and one draw needn't show every extreme that they name: `segments`: segment numbers start at 0 in every block of 1536 tokens along the token dimension and never fall within it; each item holds 258 or 1026 tokens, except that the last item of a block may be cut short.
All inputs are finite; a program needn't handle non-finite values.
Results may differ from the reference program's by a relative error of at most 0.023.
The reference program's roundings to bfloat16 on the way count: a program that leaves them out, or rounds other values in their place, can miss the bound.
Values may be sent and summed in bfloat16 or wider, within the bound.
No kernel may reach another device: no remote copies, remote signals or barrier semaphores. Data moves between devices by JAX's collectives and lax.ppermute only.
A program may use at most 384 MiB of HBM per device.

```python
import jax
import jax.numpy as jnp
from jax import lax

D = 1152
HEADS = 16
HEAD_DIM = 72
FF = 4608
TOK_MB = 1536
MB = 2
SHORT_ITEM = 258
LONG_ITEM = 1026
TOKENS = 24576
N_DP = 16


def draw_segments(key, part):
    item_slots = TOK_MB // SHORT_ITEM + 1
    kinds = jax.random.randint(key, (MB, N_DP, item_slots), 0, 2)
    dp_position = jnp.arange(N_DP, dtype=jnp.int32)[None, :, None]
    first_item = jnp.arange(item_slots, dtype=jnp.int32)[None, None, :] == 0
    kinds = jnp.where(dp_position == 0, 0, kinds)
    kinds = jnp.where((dp_position == 1) & first_item, 1, kinds)
    item_sizes = SHORT_ITEM + kinds * (LONG_ITEM - SHORT_ITEM)
    item_ends = jnp.cumsum(item_sizes, axis=-1)
    positions = jnp.arange(TOK_MB, dtype=jnp.int32)
    passed = item_ends[:, :, None, :] <= positions[None, None, :, None]
    numbers = jnp.sum(passed.astype(jnp.int32), axis=-1)
    return numbers.reshape(MB, N_DP * TOK_MB).astype(jnp.int32)


def spiked(values, rng, source, target, blocks, factor):
    owner, partner = [(jnp.arange(values.shape[position]) // (values.shape[position] // blocks)).reshape([-1 if axis == position else 1 for axis in range(values.ndim)]) for position in (source, target)]
    chosen = jax.random.permutation(rng, blocks)[partner]
    strong = (owner == chosen) | (owner == (partner + blocks // 2) % blocks)
    return jnp.where(strong, factor * values, values)


def block_levels(key, dims, cuts, low, top_value):
    level, own = 1.0, jax.random.fold_in(key, 6)
    for axis_at, parts in cuts:
        draws = jnp.exp(jax.random.uniform(jax.random.fold_in(own, axis_at), (parts,), jnp.float32, low / len(cuts), top_value / len(cuts)))
        level = level * jnp.repeat(draws, dims[axis_at] // parts).reshape([-1 if axis == axis_at else 1 for axis in range(len(dims))])
    return level


def scatter_about(stream_key, extent, deviation, reach, shards=(), held_as=jnp.bfloat16):
    level = block_levels(stream_key, extent, shards, -0.22, 0.18) if shards else 1.0
    drawn = jax.random.normal(stream_key, extent, jnp.float32) * deviation * level
    return jnp.minimum(jnp.maximum(drawn, -reach), reach).astype(held_as)


def gaussian_with(stream_key, shape, width, most, shards, heavy, kind=jnp.bfloat16):
    array = width * jax.random.normal(stream_key, shape, jnp.float32)
    if shards:
        array = array * block_levels(stream_key, shape, shards, -0.22, 0.18)
    return jnp.clip(spiked(array, jax.random.fold_in(stream_key, 3), *heavy), -most, most).astype(kind)


def setup_inputs(seed: int = 0) -> dict:
    seeds = jax.random.split(jax.random.key(seed), 18)
    return {
        "layer_input": scatter_about(seeds[0], (MB, TOKENS, D), 1.0, 6.0, ((1, 16), (2, 2))),
        "skip_input": scatter_about(seeds[1], (MB, TOKENS, D), 1.0, 6.0, ((1, 16), (2, 2))),
        "segments": draw_segments(jax.random.fold_in(seeds[17], 71), 0),
        "skip_weight": scatter_about(seeds[3], (2, D, D), (2 * D) ** -0.5, 0.125, ((1, 2),)),
        "skip_bias": scatter_about(seeds[4], (D,), 0.3, 1.796875),
        "attn_norm_gain": jnp.clip(1.0 + 0.15 * jax.random.normal(seeds[5], (D,), jnp.float32), 0.25, 1.75).astype(jnp.bfloat16),
        "attn_norm_bias": scatter_about(seeds[6], (D,), 0.3, 1.796875),
        "qkv_weight": scatter_about(seeds[7], (D, 3, D), (D // 2) ** -0.5, 0.25, ((2, 2),)),
        "proj_weight": scatter_about(seeds[8], (D, D), (D // 4) ** -0.5, 0.375, ((0, 2),)),
        "proj_bias": scatter_about(seeds[9], (D,), 0.3, 1.796875),
        "mlp_norm_gain": jnp.clip(1.0 + 0.15 * jax.random.normal(seeds[10], (D,), jnp.float32), 0.25, 1.75).astype(jnp.bfloat16),
        "mlp_norm_bias": scatter_about(seeds[11], (D,), 0.3, 1.796875),
        "up_weight": scatter_about(seeds[12], (D, FF), D ** -0.5, 0.1875, ((1, 2),)),
        "up_bias": scatter_about(seeds[13], (FF,), 0.5, 3.0, ((0, 2),)),
        "down_weight": scatter_about(seeds[14], (FF, D), (FF // 2) ** -0.5, 0.125, ((0, 2),)),
        "down_bias": scatter_about(seeds[15], (D,), 0.3, 1.796875),
        "cotangent": gaussian_with(seeds[16], (MB, TOKENS, D), 1.0, 6.0, ((1, 32),), (1, 2, 32, 2.75)),
    }


norm_eps = 1e-05
masked_score = -1e+30

@jax.custom_vjp
def low(v):
    return lax.optimization_barrier(v.astype(jnp.bfloat16)).astype(jnp.float32)

@jax.custom_vjp
def low_back(v):
    return v

def low_keep(v):
    return (low(v), None)

def low_pass(kept, grad):
    return (grad,)

def back_keep(v):
    return (v, None)

def back_low(kept, grad):
    return (low(grad),)
low.defvjp(low_keep, low_pass)
low_back.defvjp(back_keep, back_low)

def matmul(left, right):
    return jnp.dot(left, right, precision=lax.Precision.HIGHEST)

def layer_norm(hidden, gain, shift):
    center = hidden - lax.optimization_barrier(jnp.mean(hidden, axis=-1, keepdims=True))
    spread = lax.optimization_barrier(jnp.mean(center * center, axis=-1, keepdims=True))
    return center * lax.rsqrt(spread + norm_eps) * gain + shift

def pack_forward(params, pack_input, pack_skip, pack_segments):
    skip_weight, skip_bias, attn_norm_gain, attn_norm_bias, qkv_weight, proj_weight, proj_bias, mlp_norm_gain, mlp_norm_bias, up_weight, up_bias, down_weight, down_bias = params
    length = pack_input.shape[0]
    base = low_back(matmul(pack_input, skip_weight[0]) + matmul(pack_skip, skip_weight[1]) + skip_bias)
    first = low(layer_norm(base, attn_norm_gain, attn_norm_bias))
    projected = low_back(low(matmul(first, qkv_weight.reshape(D, 3 * D))))
    queries = projected[:, :D].reshape(length, HEADS, HEAD_DIM)
    keys_all = projected[:, D:2 * D].reshape(length, HEADS, HEAD_DIM)
    values_all = projected[:, 2 * D:].reshape(length, HEADS, HEAD_DIM)
    block_rows = min(512, length)
    blocks = length // block_rows
    score_scale = HEAD_DIM ** (-0.5)

    def attend_block(operands):
        query_block, segment_block = operands
        scores = jnp.einsum('qhd,khd->hqk', query_block, keys_all, precision=lax.Precision.HIGHEST) * score_scale
        same_item = segment_block[:, None] == pack_segments[None, :]
        scores = low_back(jnp.where(same_item[None], scores, masked_score))
        weights = low(jax.nn.softmax(scores, axis=-1))
        return jnp.einsum('hqk,khd->qhd', weights, values_all, precision=lax.Precision.HIGHEST)
    attended = lax.map(jax.checkpoint(attend_block), (queries.reshape(blocks, block_rows, HEADS, HEAD_DIM), pack_segments.reshape(blocks, block_rows)))
    mixture = low_back(low(attended.reshape(length, D)))
    middle = base + low_back(matmul(mixture, proj_weight) + proj_bias)
    second = low(layer_norm(middle, mlp_norm_gain, mlp_norm_bias))
    before = low_back(matmul(second, up_weight) + up_bias)
    hidden = low(jax.nn.gelu(before, approximate=False))
    return middle + (matmul(hidden, down_weight) + down_bias)

def add_grads(total_grad, new_grad):
    return total_grad + new_grad

def reference(layer_input, skip_input, segments, skip_weight, skip_bias, attn_norm_gain, attn_norm_bias, qkv_weight, proj_weight, proj_bias, mlp_norm_gain, mlp_norm_bias, up_weight, up_bias, down_weight, down_bias, cotangent):
    params = tuple((weight.astype(jnp.float32) for weight in (skip_weight, skip_bias, attn_norm_gain, attn_norm_bias, qkv_weight, proj_weight, proj_bias, mlp_norm_gain, mlp_norm_bias, up_weight, up_bias, down_weight, down_bias)))
    packs = MB * N_DP
    pack_inputs = layer_input.astype(jnp.float32).reshape(packs, TOK_MB, D)
    pack_skips = skip_input.astype(jnp.float32).reshape(packs, TOK_MB, D)
    pack_segs = segments.reshape(packs, TOK_MB)
    pack_cots = cotangent.astype(jnp.float32).reshape(packs, TOK_MB, D)

    def step_pack(totals, operands):
        pack_input, pack_skip, pack_segment, pack_cot = operands

        def forward_only(weights_all, inputs_now, skips_now):
            return pack_forward(weights_all, inputs_now, skips_now, pack_segment)
        produced, pullback = jax.vjp(forward_only, params, pack_input, pack_skip)
        grad_params, grad_input, grad_skip = pullback(pack_cot)
        totals = jax.tree.map(add_grads, totals, grad_params)
        return (totals, (produced.astype(jnp.bfloat16), grad_input.astype(jnp.bfloat16), grad_skip.astype(jnp.bfloat16)))
    zero_grads = jax.tree.map(jnp.zeros_like, params)
    totals, (produced, grad_inputs, grad_skips) = lax.scan(step_pack, zero_grads, (pack_inputs, pack_skips, pack_segs, pack_cots))
    grad_scale = (MB * TOKENS) ** (-0.5)
    scaled = tuple((total * grad_scale for total in totals))
    return (produced.reshape(MB, TOKENS, D), grad_inputs.reshape(MB, TOKENS, D), grad_skips.reshape(MB, TOKENS, D), scaled[0], scaled[1], scaled[2], scaled[3], scaled[4], scaled[5], scaled[6], scaled[7], scaled[8], scaled[9], scaled[10], scaled[11], scaled[12])
```

```python
import functools
import math

import jax
import jax.numpy as jnp
from jax import lax
from jax.experimental import pallas as pl
from jax.experimental.pallas import tpu as pltpu
from jax.sharding import PartitionSpec as P

HEAD_DIM = 72
LOG2E = 1.4426950408889634
TILE_ROWS = 512
TILE_KEYS = 256
TILE_HEADS = 2


norm_eps = 1e-05
masked_score = -1e30


def normalize(hidden, gain, shift):
    center = hidden - jnp.mean(hidden, axis=-1, keepdims=True)
    spread = jnp.mean(center * center, axis=-1, keepdims=True)
    inverse = lax.rsqrt(spread + norm_eps)
    scaled = center * inverse
    return (scaled * gain + shift, scaled, inverse)


def normalize_back(grad_out, scaled, inverse, gain):
    grad_scaled = grad_out * gain
    centered = grad_scaled - jnp.mean(grad_scaled, axis=-1, keepdims=True)
    return inverse * (centered - scaled * jnp.mean(grad_scaled * scaled, axis=-1, keepdims=True))


def gelu_slope(before):
    return (
        0.5 * (1.0 + lax.erf(before * 0.7071067811865476))
        + before * jnp.exp(-0.5 * before * before) * 0.3989422804014327
    )


def transposed_left(left, right):
    return lax.dot_general(
        left, right, (((0,), (0,)), ((), ())), preferred_element_type=jnp.float32
    )


def transposed_right(left, right):
    return lax.dot_general(
        left, right, (((1,), (1,)), ((), ())), preferred_element_type=jnp.float32
    )


def key_ranges(segment_ids, rows, block):
    length = segment_ids.shape[0]
    starts = segment_ids[::rows]
    ends = segment_ids[rows - 1 :: rows]
    low = jnp.sum((segment_ids[None] < starts[:, None]).astype(jnp.int32), axis=1)
    high = jnp.sum((segment_ids[None] <= ends[:, None]).astype(jnp.int32), axis=1)
    return jnp.concatenate([low // block, (high + block - 1) // block])

def attend_kernel(rows, block, range_ref, seg_row_ref, seg_col_ref, packed_ref, mixed_ref, total_ref, key_ref):
    heads, length = packed_ref.shape[1], packed_ref.shape[3]
    tiles = length // rows
    factor = HEAD_DIM**-0.5 * LOG2E
    for h in range(heads):
        key_ref[h] = packed_ref[1, h].T

    def query_step(tile, carry):
        at = pl.ds(pl.multiple_of(tile * rows, rows), rows)
        seg_query = seg_row_ref[:, at]
        queries = [packed_ref[0, h, :, at] for h in range(heads)]

        def key_step(key_tile, state):
            keys_at = pl.ds(pl.multiple_of(key_tile * block, block), block)
            same = seg_col_ref[keys_at, :] == seg_query
            fresh = []
            for h in range(heads):
                highest, total, mixed = state[3 * h : 3 * h + 3]
                scores = jnp.dot(key_ref[h, keys_at, :], queries[h], preferred_element_type=jnp.float32)
                scores = jnp.where(same, scores, masked_score)
                top = jnp.maximum(highest, jnp.max(scores, axis=0, keepdims=True))
                powers = jnp.exp2((scores - top) * factor)
                fade = jnp.exp2((highest - top) * factor)
                total = total * fade + jnp.sum(powers, axis=0, keepdims=True)
                mixed = mixed * fade + jnp.dot(
                    packed_ref[2, h, :, keys_at], powers.astype(jnp.bfloat16), preferred_element_type=jnp.float32
                )
                fresh += [top, total, mixed]
            return tuple(fresh)

        start = []
        for h in range(heads):
            start += [
                jnp.full((1, rows), masked_score, jnp.float32),
                jnp.zeros((1, rows), jnp.float32),
                jnp.zeros((HEAD_DIM, rows), jnp.float32),
            ]
        state = lax.fori_loop(range_ref[tile], range_ref[tiles + tile], key_step, tuple(start))
        for h in range(heads):
            highest, total, mixed = state[3 * h : 3 * h + 3]
            mixed_ref[h, :, at] = (mixed / total).astype(jnp.bfloat16)
            total_ref[0, h : h + 1, at] = highest * factor + jnp.log2(total)
        return carry

    lax.fori_loop(0, tiles, query_step, 0)

def attend_back_kernel(rows, block, range_ref, seg_row_ref, seg_col_ref, packed_ref, mixed_ref, grad_ref, total_ref,
                       out_ref, query_ref, key_ref, value_ref, grad_t_ref, grad_key_ref, grad_value_ref):
    heads, length = packed_ref.shape[1], packed_ref.shape[3]
    tiles = length // rows
    scale = HEAD_DIM**-0.5
    factor = scale * LOG2E
    for h in range(heads):
        query_ref[h] = packed_ref[0, h].T
        key_ref[h] = packed_ref[1, h].T
        value_ref[h] = packed_ref[2, h].T
        grad_t_ref[h] = grad_ref[h].T
    grad_key_ref[...] = jnp.zeros_like(grad_key_ref)
    grad_value_ref[...] = jnp.zeros_like(grad_value_ref)

    def query_step(tile, carry):
        at = pl.ds(pl.multiple_of(tile * rows, rows), rows)
        seg_query = seg_row_ref[:, at]
        inner = [
            jnp.sum(grad_ref[h, :, at].astype(jnp.float32) * mixed_ref[h, :, at].astype(jnp.float32), axis=0, keepdims=True)
            for h in range(heads)
        ]
        totals = [total_ref[0, h : h + 1, at] for h in range(heads)]

        def key_step(key_tile, state):
            keys_at = pl.ds(pl.multiple_of(key_tile * block, block), block)
            same = seg_col_ref[keys_at, :] == seg_query
            fresh = []
            for h in range(heads):
                scores = jnp.dot(key_ref[h, keys_at, :], packed_ref[0, h, :, at], preferred_element_type=jnp.float32)
                probs = jnp.where(same, jnp.exp2(scores * factor - totals[h]), 0.0)
                grad_probs = jnp.dot(value_ref[h, keys_at, :], grad_ref[h, :, at], preferred_element_type=jnp.float32)
                grad_scores = (probs * (grad_probs - inner[h])).astype(jnp.bfloat16)
                grad_value_ref[h, keys_at, :] += jnp.dot(
                    probs.astype(jnp.bfloat16), grad_t_ref[h, at, :], preferred_element_type=jnp.float32
                )
                grad_key_ref[h, keys_at, :] += jnp.dot(
                    grad_scores, query_ref[h, at, :], preferred_element_type=jnp.float32
                )
                fresh.append(
                    state[h] + jnp.dot(packed_ref[1, h, :, keys_at], grad_scores, preferred_element_type=jnp.float32)
                )
            return tuple(fresh)

        state = lax.fori_loop(
            range_ref[tile], range_ref[tiles + tile], key_step,
            tuple(jnp.zeros((HEAD_DIM, rows), jnp.float32) for _ in range(heads)),
        )
        for h in range(heads):
            out_ref[0, h, :, at] = (state[h] * scale).astype(jnp.bfloat16)
        return carry

    lax.fori_loop(0, tiles, query_step, 0)
    for h in range(heads):
        out_ref[1, h] = (grad_key_ref[h] * scale).T.astype(jnp.bfloat16)
        out_ref[2, h] = grad_value_ref[h].T.astype(jnp.bfloat16)

def attend_tables(segment_ids):
    length = segment_ids.shape[0]
    rows = math.gcd(length, TILE_ROWS)
    ranges = key_ranges(segment_ids, rows, math.gcd(length, TILE_KEYS))
    return ranges, segment_ids[None], jnp.broadcast_to(segment_ids[:, None], (length, rows))


def attend(packed, ranges, seg_row, seg_col):
    _, heads, _, length = packed.shape
    rows, block, group = seg_col.shape[1], math.gcd(length, TILE_KEYS), math.gcd(heads, TILE_HEADS)
    area = heads * length * length
    return pl.pallas_call(
        functools.partial(attend_kernel, rows, block),
        grid_spec=pltpu.PrefetchScalarGridSpec(
            num_scalar_prefetch=1,
            grid=(heads // group,),
            in_specs=[
                pl.BlockSpec((1, length), lambda g, r: (0, 0)),
                pl.BlockSpec((length, rows), lambda g, r: (0, 0)),
                pl.BlockSpec((3, group, HEAD_DIM, length), lambda g, r: (0, g, 0, 0)),
            ],
            out_specs=[
                pl.BlockSpec((group, HEAD_DIM, length), lambda g, r: (g, 0, 0)),
                pl.BlockSpec((1, group, length), lambda g, r: (g, 0, 0)),
            ],
            scratch_shapes=[pltpu.VMEM((group, length, HEAD_DIM), jnp.bfloat16)],
        ),
        out_shape=[
            jax.ShapeDtypeStruct((heads, HEAD_DIM, length), jnp.bfloat16),
            jax.ShapeDtypeStruct((heads // group, group, length), jnp.float32),
        ],
        cost_estimate=pl.CostEstimate(flops=4 * area * 128, transcendentals=area, bytes_accessed=8 * heads * HEAD_DIM * length),
        name="attend",
    )(ranges, seg_row, seg_col, packed)

def attend_back(packed, mixed, grad, totals, ranges, seg_row, seg_col):
    _, heads, _, length = packed.shape
    rows, block, group = seg_col.shape[1], math.gcd(length, TILE_KEYS), math.gcd(heads, TILE_HEADS)
    area = heads * length * length
    return pl.pallas_call(
        functools.partial(attend_back_kernel, rows, block),
        grid_spec=pltpu.PrefetchScalarGridSpec(
            num_scalar_prefetch=1,
            grid=(heads // group,),
            in_specs=[
                pl.BlockSpec((1, length), lambda g, r: (0, 0)),
                pl.BlockSpec((length, rows), lambda g, r: (0, 0)),
                pl.BlockSpec((3, group, HEAD_DIM, length), lambda g, r: (0, g, 0, 0)),
                pl.BlockSpec((group, HEAD_DIM, length), lambda g, r: (g, 0, 0)),
                pl.BlockSpec((group, HEAD_DIM, length), lambda g, r: (g, 0, 0)),
                pl.BlockSpec((1, group, length), lambda g, r: (g, 0, 0)),
            ],
            out_specs=pl.BlockSpec((3, group, HEAD_DIM, length), lambda g, r: (0, g, 0, 0)),
            scratch_shapes=[pltpu.VMEM((group, length, HEAD_DIM), jnp.bfloat16)] * 4
            + [pltpu.VMEM((group, length, HEAD_DIM), jnp.float32)] * 2,
        ),
        out_shape=jax.ShapeDtypeStruct(packed.shape, jnp.bfloat16),
        cost_estimate=pl.CostEstimate(flops=10 * area * 128, transcendentals=area, bytes_accessed=16 * heads * HEAD_DIM * length),
        name="attend_back",
    )(ranges, seg_row, seg_col, packed, mixed, grad, totals)


def split_layer(
    layer_input,
    skip_input,
    segments,
    skip_weight,
    skip_bias,
    attn_norm_gain,
    attn_norm_bias,
    qkv_weight,
    proj_weight,
    proj_bias,
    mlp_norm_gain,
    mlp_norm_bias,
    up_weight,
    up_bias,
    down_weight,
    down_bias,
    cotangent,
):
    micro, length, part_width = layer_input.shape
    width = skip_bias.shape[0]
    hidden_part = up_bias.shape[0]
    model_count = lax.axis_size("mp")
    data_count = lax.axis_size("dp")
    head_count = part_width // HEAD_DIM
    qkv_local = qkv_weight.reshape(width, 3 * part_width)
    grad_skip = jnp.zeros((2, part_width, width), jnp.float32)
    grad_qkv = jnp.zeros((width, 3 * part_width), jnp.float32)
    grad_proj = jnp.zeros((part_width, width), jnp.float32)
    vector_totals = jnp.zeros((7, width), jnp.float32)
    grad_up = jnp.zeros((width, hidden_part), jnp.float32)
    grad_down = jnp.zeros((hidden_part, width), jnp.float32)
    grad_up_bias = jnp.zeros((hidden_part,), jnp.float32)
    results = []
    input_grads = []
    skip_grads = []
    for micro_step in range(micro):
        local_input = layer_input[micro_step]
        local_skip = skip_input[micro_step]
        segment_ids = segments[micro_step]
        grad_output = cotangent[micro_step]
        grad_float = grad_output.astype(jnp.float32)
        base = (
            lax.psum_scatter(
                jnp.dot(local_input, skip_weight[0], preferred_element_type=jnp.float32)
                + jnp.dot(local_skip, skip_weight[1], preferred_element_type=jnp.float32),
                "mp",
                scatter_dimension=0,
                tiled=True,
            )
            + skip_bias
        )
        first_out, first_scaled, first_inverse = normalize(base, attn_norm_gain, attn_norm_bias)
        first_full = lax.all_gather(first_out.astype(jnp.bfloat16), "mp", axis=0, tiled=True)
        tables = attend_tables(segment_ids)
        packed = (
            lax.dot_general(
                qkv_local, first_full, (((0,), (1,)), ((), ())), preferred_element_type=jnp.float32
            )
            .astype(jnp.bfloat16)
            .reshape(3, head_count, HEAD_DIM, length)
        )
        mixed, log_totals = attend(packed, *tables)
        mixture = mixed.reshape(part_width, length).T
        middle = base + (
            lax.psum_scatter(
                jnp.dot(mixture, proj_weight, preferred_element_type=jnp.float32).astype(
                    jnp.bfloat16
                ),
                "mp",
                scatter_dimension=0,
                tiled=True,
            ).astype(jnp.float32)
            + proj_bias
        )
        second_out, second_scaled, second_inverse = normalize(middle, mlp_norm_gain, mlp_norm_bias)
        second_low = second_out.astype(jnp.bfloat16)
        second_full = lax.all_gather(second_low, "mp", axis=0, tiled=True)
        before = jnp.dot(second_full, up_weight, preferred_element_type=jnp.float32) + up_bias
        hidden = jax.nn.gelu(before, approximate=False).astype(jnp.bfloat16)
        result = middle + (
            lax.psum_scatter(
                jnp.dot(hidden, down_weight, preferred_element_type=jnp.float32).astype(
                    jnp.bfloat16
                ),
                "mp",
                scatter_dimension=0,
                tiled=True,
            ).astype(jnp.float32)
            + down_bias
        )
        grad_full = lax.all_gather(grad_output, "mp", axis=0, tiled=True)
        grad_hidden = transposed_right(grad_full, down_weight)
        grad_before = (grad_hidden * gelu_slope(before)).astype(jnp.bfloat16)
        grad_down = grad_down + transposed_left(hidden, grad_full)
        grad_up = grad_up + transposed_left(second_full, grad_before)
        grad_up_bias = grad_up_bias + jnp.sum(grad_before.astype(jnp.float32), axis=0)
        grad_second = lax.psum_scatter(
            transposed_right(grad_before, up_weight).astype(jnp.bfloat16),
            "mp",
            scatter_dimension=0,
            tiled=True,
        ).astype(jnp.float32)
        results.append(result.astype(jnp.bfloat16))
        grad_middle = grad_float + normalize_back(
            grad_second, second_scaled, second_inverse, mlp_norm_gain
        )
        grad_branch = grad_middle.astype(jnp.bfloat16)
        grad_attn_full = lax.all_gather(grad_branch, "mp", axis=0, tiled=True)
        grad_proj = grad_proj + transposed_left(mixture, grad_attn_full)
        grad_mixture = transposed_right(proj_weight, grad_attn_full).astype(jnp.bfloat16)
        grad_packed = attend_back(
            packed, mixed, grad_mixture.reshape(head_count, HEAD_DIM, length), log_totals, *tables
        )
        grad_projected = grad_packed.reshape(3 * part_width, length).T
        grad_qkv = grad_qkv + transposed_left(first_full, grad_projected)
        grad_first = lax.psum_scatter(
            transposed_right(grad_projected, qkv_local).astype(jnp.bfloat16),
            "mp",
            scatter_dimension=0,
            tiled=True,
        ).astype(jnp.float32)
        grad_base = grad_middle + normalize_back(
            grad_first, first_scaled, first_inverse, attn_norm_gain
        )
        grad_base_low = grad_base.astype(jnp.bfloat16)
        grad_base_full = lax.all_gather(grad_base_low, "mp", axis=0, tiled=True)
        grad_skip = grad_skip + jnp.stack(
            [
                transposed_left(local_input, grad_base_full),
                transposed_left(local_skip, grad_base_full),
            ]
        )
        input_grads.append(transposed_right(grad_base_full, skip_weight[0]).astype(jnp.bfloat16))
        skip_grads.append(transposed_right(grad_base_full, skip_weight[1]).astype(jnp.bfloat16))
        vector_totals = vector_totals + jnp.stack(
            [
                jnp.sum(grad_base_low.astype(jnp.float32), axis=0),
                jnp.sum(grad_first * first_scaled, axis=0),
                jnp.sum(grad_first, axis=0),
                jnp.sum(grad_branch.astype(jnp.float32), axis=0),
                jnp.sum(grad_second * second_scaled, axis=0),
                jnp.sum(grad_second, axis=0),
                jnp.sum(grad_float, axis=0),
            ]
        )
    grad_scale = (micro * length * data_count) ** (-0.5)
    up_bias_vector = lax.dynamic_update_slice(
        jnp.zeros((hidden_part * model_count,), jnp.float32),
        grad_up_bias,
        (lax.axis_index("mp") * hidden_part,),
    )
    vector_sums, up_bias_sum = lax.psum((vector_totals, up_bias_vector), ("dp", "mp"))
    skip_share, qkv_share, proj_share, up_share, down_share = (
        lax.psum_scatter(
            grad_skip.astype(jnp.bfloat16), "dp", scatter_dimension=2, tiled=True
        ).astype(jnp.float32),
        lax.psum_scatter(
            grad_qkv.reshape(width, 3, part_width).astype(jnp.bfloat16),
            "dp",
            scatter_dimension=0,
            tiled=True,
        ).astype(jnp.float32),
        lax.psum_scatter(
            grad_proj.astype(jnp.bfloat16), "dp", scatter_dimension=1, tiled=True
        ).astype(jnp.float32),
        lax.psum_scatter(
            grad_up.astype(jnp.bfloat16), "dp", scatter_dimension=0, tiled=True
        ).astype(jnp.float32),
        lax.psum_scatter(
            grad_down.astype(jnp.bfloat16), "dp", scatter_dimension=1, tiled=True
        ).astype(jnp.float32),
    )
    return (
        jnp.stack(results),
        jnp.stack(input_grads),
        jnp.stack(skip_grads),
        skip_share * grad_scale,
        vector_sums[0] * grad_scale,
        vector_sums[1] * grad_scale,
        vector_sums[2] * grad_scale,
        qkv_share * grad_scale,
        proj_share * grad_scale,
        vector_sums[3] * grad_scale,
        vector_sums[4] * grad_scale,
        vector_sums[5] * grad_scale,
        up_share * grad_scale,
        up_bias_sum * grad_scale,
        down_share * grad_scale,
        vector_sums[6] * grad_scale,
    )


def swap_axis(value):
    return lax.ppermute(value, "mp", [(0, 1), (1, 0)])


def swap_bit(value, bit):
    count = lax.axis_size("dp")
    return lax.ppermute(value, "dp", [(index, index ^ bit) for index in range(count)])


def pick(value, index, axis=0):
    return lax.dynamic_index_in_dim(value, index, axis, keepdims=False)


def fetch_half(weight, place):
    rows = weight.shape[0] // 4
    at = place & 3
    near = swap_axis(lax.dynamic_slice_in_dim(weight, at * rows, rows))
    side = swap_bit(near, 2)
    whole = jnp.zeros_like(weight)
    pieces = ((near, at), (side, at ^ 2), (swap_bit(near, 1), at ^ 1), (swap_bit(side, 1), at ^ 3))
    for piece, slot in pieces:
        whole = lax.dynamic_update_slice_in_dim(whole, piece, slot * rows, 0)
    return whole


def add_low(left, right):
    return (left.astype(jnp.float32) + right.astype(jnp.float32)).astype(jnp.bfloat16)


def halve(values, axis, bit, place):
    mine = (place // bit) & 1
    return [add_low(pick(v, mine, axis), swap_bit(pick(v, 1 - mine, axis), bit)) for v in values]


def reduce_pair(own, other, place):
    depth, columns = own.shape
    shards = [v.reshape(2, 2, 2, 2, depth // 16, columns) for v in (own, other)]
    shards = halve(shards, 3, 1, place)
    shards = halve(shards, 2, 2, place)
    total = [add_low(shards[0], swap_axis(shards[1]))]
    total = halve(total, 1, 4, place)
    return halve(total, 0, 8, place)[0].astype(jnp.float32)


def sum_everywhere(value):
    for bit in (1, 2, 4, 8):
        value = value + swap_bit(value, bit)
    return value + swap_axis(value)


def after(value, *earlier):
    return lax.optimization_barrier((value, *earlier))[0]


def whole_layer(
    layer_input,
    skip_input,
    segments,
    skip_weight,
    skip_bias,
    attn_norm_gain,
    attn_norm_bias,
    qkv_weight,
    proj_weight,
    proj_bias,
    mlp_norm_gain,
    mlp_norm_bias,
    up_weight,
    up_bias,
    down_weight,
    down_bias,
    cotangent,
):
    micro, length, part = layer_input.shape
    width = skip_bias.shape[0]
    hidden_part = up_bias.shape[0]
    heads = part // HEAD_DIM
    rows_half = length // 2
    low = jnp.bfloat16
    mine = lax.axis_index("mp")
    place = lax.axis_index("dp")
    first_half = mine == 0

    def ordered(own, other, axis):
        return jnp.where(
            first_half, jnp.concatenate([own, other], axis), jnp.concatenate([other, own], axis)
        )

    pairs = jnp.concatenate([layer_input, skip_input], axis=2)
    pair_own = pick(pairs, mine)
    pair_other = swap_axis(pick(pairs, 1 - mine))
    skip_own = skip_weight.reshape(2 * part, width)
    skip_other = fetch_half(skip_own, place)
    qkv_own = qkv_weight.reshape(width, 3 * part)
    qkv_other = fetch_half(qkv_own, place)
    proj_other = fetch_half(proj_weight, place)
    up_other = fetch_half(up_weight, place)
    up_bias_other = swap_axis(up_bias)
    down_other = fetch_half(down_weight, place)
    grad_out = ordered(pick(cotangent, mine), swap_axis(pick(cotangent, 1 - mine)), 0)
    segment_ids = pick(segments, mine)
    tables = attend_tables(segment_ids)

    def dot(left, right):
        return jnp.dot(left, right, preferred_element_type=jnp.float32)

    base = dot(pair_own, skip_own) + dot(pair_other, skip_other) + skip_bias
    first_out, first_scaled, first_inverse = normalize(base, attn_norm_gain, attn_norm_bias)
    first = first_out.astype(low)
    mixture, middle = [], base
    saved = []
    for weight, proj in ((qkv_own, proj_weight), (qkv_other, proj_other)):
        packed = (
            lax.dot_general(weight, first, (((0,), (1,)), ((), ())), preferred_element_type=jnp.float32)
            .astype(low)
            .reshape(3, heads, HEAD_DIM, length)
        )
        mixed, totals = attend(packed, *tables)
        saved.append((packed, mixed, totals))
        middle = middle + transposed_left(mixed.reshape(part, length), proj)
    middle = middle + proj_bias
    second_out, second_scaled, second_inverse = normalize(middle, mlp_norm_gain, mlp_norm_bias)
    second = second_out.astype(low)
    result = middle
    hidden, slope = [], []
    for up, bias, down in ((up_weight, up_bias, down_weight), (up_other, up_bias_other, down_other)):
        before = dot(second, up) + bias
        hidden.append(jax.nn.gelu(before, approximate=False).astype(low))
        slope.append(gelu_slope(before).astype(low))
        result = result + dot(hidden[-1], down)
    result = (result + down_bias).astype(low).reshape(2, rows_half, width)
    layer_output = ordered(pick(result, mine)[None], swap_axis(pick(result, 1 - mine))[None], 0)

    grad_second, up_grads, down_grads, up_bias_grads = 0.0, [], [], []
    for up, down, bent, act in (
        (up_weight, down_weight, slope[0], hidden[0]),
        (up_other, down_other, slope[1], hidden[1]),
    ):
        down_grads.append(transposed_left(grad_out, act).astype(low))
        grad_before = (transposed_right(grad_out, down) * bent.astype(jnp.float32)).astype(low)
        up_grads.append(transposed_left(second, grad_before).astype(low))
        up_bias_grads.append(jnp.sum(grad_before.astype(jnp.float32), axis=0))
        grad_second = grad_second + transposed_right(grad_before, up)
    down_share = reduce_pair(*down_grads, place)
    up_share = reduce_pair(*up_grads, place)

    grad_float = grad_out.astype(jnp.float32)
    grad_middle = grad_float + normalize_back(grad_second, second_scaled, second_inverse, mlp_norm_gain)
    grad_branch = grad_middle.astype(low)
    early = sum_everywhere(
        jnp.concatenate(
            [
                jnp.sum(grad_branch.astype(jnp.float32), axis=0),
                jnp.sum(grad_second * second_scaled, axis=0),
                jnp.sum(grad_second, axis=0),
                jnp.sum(grad_float, axis=0),
                ordered(*up_bias_grads, 0),
            ]
        )
    )
    grad_first, qkv_grads, proj_grads = 0.0, [], []
    for (packed, mixed, totals), weight, proj in (
        (saved[0], qkv_own, proj_weight),
        (saved[1], qkv_other, proj_other),
    ):
        grad_mixture = transposed_right(proj, grad_branch).astype(low).reshape(heads, HEAD_DIM, length)
        flat = mixed.reshape(part, length)
        proj_grads.append(
            lax.dot_general(
                grad_branch, flat, (((0,), (1,)), ((), ())), preferred_element_type=jnp.float32
            ).astype(low)
        )
        grad_packed = attend_back(packed, mixed, grad_mixture, totals, *tables).reshape(3 * part, length)
        qkv_grads.append(
            lax.dot_general(
                first, grad_packed, (((0,), (1,)), ((), ())), preferred_element_type=jnp.float32
            ).astype(low)
        )
        grad_first = grad_first + lax.dot_general(
            grad_packed, weight, (((0,), (1,)), ((), ())), preferred_element_type=jnp.float32
        )
    proj_share = reduce_pair(*proj_grads, place)
    qkv_share = reduce_pair(*qkv_grads, place)
    grad_base = (
        grad_middle + normalize_back(grad_first, first_scaled, first_inverse, attn_norm_gain)
    ).astype(low)
    input_grad, skip_grad = (
        ordered(
            transposed_right(grad_base, skip_weight[side]).astype(low)[None],
            swap_axis(
                transposed_right(grad_base, skip_other[side * part : (side + 1) * part]).astype(low)
            )[None],
            0,
        )
        for side in range(2)
    )
    skip_share = reduce_pair(
        transposed_left(grad_base, pair_own).astype(low),
        transposed_left(grad_base, pair_other).astype(low),
        place,
    )
    late = sum_everywhere(
        jnp.concatenate(
            [
                jnp.sum(grad_base.astype(jnp.float32), axis=0),
                jnp.sum(grad_first * first_scaled, axis=0),
                jnp.sum(grad_first, axis=0),
            ]
        )
    )
    grad_scale = (micro * length * lax.axis_size("dp")) ** (-0.5)
    late = (late * grad_scale).reshape(3, width)
    early = early * grad_scale
    vectors = early[: 4 * width].reshape(4, width)
    return (
        layer_output,
        input_grad,
        skip_grad,
        skip_share.T.reshape(2, part, -1) * grad_scale,
        late[0],
        late[1],
        late[2],
        qkv_share.reshape(-1, 3, part) * grad_scale,
        proj_share.T * grad_scale,
        vectors[0],
        vectors[1],
        vectors[2],
        up_share * grad_scale,
        early[4 * width :],
        down_share.T * grad_scale,
        vectors[3],
    )


def body(*arrays):
    micro, _, part = arrays[0].shape
    if lax.axis_size("mp") == micro == 2 and lax.axis_size("dp") == 16:
        return whole_layer(*arrays)
    return split_layer(*arrays)


def solution(mesh):
    return jax.shard_map(
        body,
        mesh=mesh,
        in_specs=(
            P(None, "dp", "mp"),
            P(None, "dp", "mp"),
            P(None, "dp"),
            P(None, "mp", None),
            P(),
            P(),
            P(),
            P(None, None, "mp"),
            P("mp", None),
            P(),
            P(),
            P(),
            P(None, "mp"),
            P("mp"),
            P("mp", None),
            P(),
            P(None, ("dp", "mp"), None),
        ),
        out_specs=(
            P(None, ("dp", "mp"), None),
            P(None, "dp", "mp"),
            P(None, "dp", "mp"),
            P(None, "mp", "dp"),
            P(),
            P(),
            P(),
            P("dp", None, "mp"),
            P("mp", "dp"),
            P(),
            P(),
            P(),
            P("dp", "mp"),
            P(),
            P("mp", "dp"),
            P(),
        ),
        check_vma=False,
    )
```

```python
import functools
import math

import jax
import jax.numpy as jnp
from jax import lax
from jax.experimental import pallas as pl
from jax.experimental.pallas import tpu as pltpu
from jax.sharding import PartitionSpec as P

HEAD_DIM = 72
LOG2E = 1.4426950408889634
TILE_ROWS = 512
TILE_KEYS = 256
TILE_HEADS = 2


norm_eps = 1e-05
masked_score = -1e30


def normalize(hidden, gain, shift):
    center = hidden - jnp.mean(hidden, axis=-1, keepdims=True)
    spread = jnp.mean(center * center, axis=-1, keepdims=True)
    inverse = lax.rsqrt(spread + norm_eps)
    scaled = center * inverse
    return (scaled * gain + shift, scaled, inverse)


def normalize_back(grad_out, scaled, inverse, gain):
    grad_scaled = grad_out * gain
    centered = grad_scaled - jnp.mean(grad_scaled, axis=-1, keepdims=True)
    return inverse * (centered - scaled * jnp.mean(grad_scaled * scaled, axis=-1, keepdims=True))


def gelu_slope(before):
    return (
        0.5 * (1.0 + lax.erf(before * 0.7071067811865476))
        + before * jnp.exp(-0.5 * before * before) * 0.3989422804014327
    )


def transposed_left(left, right):
    return lax.dot_general(
        left, right, (((0,), (0,)), ((), ())), preferred_element_type=jnp.float32
    )


def transposed_right(left, right):
    return lax.dot_general(
        left, right, (((1,), (1,)), ((), ())), preferred_element_type=jnp.float32
    )


def key_ranges(segment_ids, rows, block):
    length = segment_ids.shape[0]
    starts = segment_ids[::rows]
    ends = segment_ids[rows - 1 :: rows]
    low = jnp.sum((segment_ids[None] < starts[:, None]).astype(jnp.int32), axis=1)
    high = jnp.sum((segment_ids[None] <= ends[:, None]).astype(jnp.int32), axis=1)
    return jnp.concatenate([low // block, (high + block - 1) // block])

def attend_kernel(rows, block, range_ref, seg_row_ref, seg_col_ref, packed_ref, mixed_ref, total_ref, key_ref, score_ref):
    heads, length = packed_ref.shape[1], packed_ref.shape[3]
    tiles = length // rows
    factor = HEAD_DIM**-0.5 * LOG2E
    for h in range(heads):
        key_ref[h] = packed_ref[1, h].T

    def query_step(tile, carry):
        at = pl.ds(pl.multiple_of(tile * rows, rows), rows)
        seg_query = seg_row_ref[:, at]
        low, high = range_ref[tile], range_ref[tiles + tile]

        def score_step(key_tile, tops):
            keys_at = pl.ds(pl.multiple_of(key_tile * block, block), block)
            same = seg_col_ref[keys_at, :] == seg_query
            fresh = []
            for h in range(heads):
                scores = jnp.dot(
                    key_ref[h, keys_at, :], packed_ref[0, h, :, at], preferred_element_type=jnp.float32
                )
                scores = jnp.where(same, scores, masked_score)
                score_ref[h, keys_at, :] = scores
                fresh.append(jnp.maximum(tops[h], jnp.max(scores, axis=0, keepdims=True)))
            return tuple(fresh)

        tops = lax.fori_loop(
            low, high, score_step, tuple(jnp.full((1, rows), masked_score, jnp.float32) for _ in range(heads))
        )
        tops = [top * factor for top in tops]

        def mix_step(key_tile, state):
            keys_at = pl.ds(pl.multiple_of(key_tile * block, block), block)
            fresh = []
            for h in range(heads):
                total, mixed = state[2 * h : 2 * h + 2]
                powers = jnp.exp2(score_ref[h, keys_at, :] * factor - tops[h])
                total = total + jnp.sum(powers, axis=0, keepdims=True)
                mixed = mixed + jnp.dot(
                    packed_ref[2, h, :, keys_at], powers.astype(jnp.bfloat16), preferred_element_type=jnp.float32
                )
                fresh += [total, mixed]
            return tuple(fresh)

        start = (jnp.zeros((1, rows), jnp.float32), jnp.zeros((HEAD_DIM, rows), jnp.float32)) * heads
        state = lax.fori_loop(low, high, mix_step, start)
        for h in range(heads):
            total, mixed = state[2 * h : 2 * h + 2]
            mixed_ref[h, :, at] = (mixed / total).astype(jnp.bfloat16)
            total_ref[0, h : h + 1, at] = tops[h] + jnp.log2(total)
        return carry

    lax.fori_loop(0, tiles, query_step, 0)

def attend_back_kernel(rows, block, range_ref, seg_row_ref, seg_col_ref, packed_ref, mixed_ref, grad_ref, total_ref,
                       out_ref, query_ref, key_ref, value_ref, grad_t_ref, grad_key_ref, grad_value_ref):
    heads, length = packed_ref.shape[1], packed_ref.shape[3]
    tiles = length // rows
    scale = HEAD_DIM**-0.5
    factor = scale * LOG2E
    for h in range(heads):
        query_ref[h] = packed_ref[0, h].T
        key_ref[h] = packed_ref[1, h].T
        value_ref[h] = packed_ref[2, h].T
        grad_t_ref[h] = grad_ref[h].T
    grad_key_ref[...] = jnp.zeros_like(grad_key_ref)
    grad_value_ref[...] = jnp.zeros_like(grad_value_ref)

    def query_step(tile, carry):
        at = pl.ds(pl.multiple_of(tile * rows, rows), rows)
        seg_query = seg_row_ref[:, at]
        inner = [
            jnp.sum(grad_ref[h, :, at].astype(jnp.float32) * mixed_ref[h, :, at].astype(jnp.float32), axis=0, keepdims=True)
            for h in range(heads)
        ]
        totals = [total_ref[0, h : h + 1, at] for h in range(heads)]

        def key_step(key_tile, state):
            keys_at = pl.ds(pl.multiple_of(key_tile * block, block), block)
            same = seg_col_ref[keys_at, :] == seg_query
            fresh = []
            for h in range(heads):
                scores = jnp.dot(key_ref[h, keys_at, :], packed_ref[0, h, :, at], preferred_element_type=jnp.float32)
                probs = jnp.where(same, jnp.exp2(scores * factor - totals[h]), 0.0)
                grad_probs = jnp.dot(value_ref[h, keys_at, :], grad_ref[h, :, at], preferred_element_type=jnp.float32)
                grad_scores = (probs * (grad_probs - inner[h])).astype(jnp.bfloat16)
                grad_value_ref[h, keys_at, :] += jnp.dot(
                    probs.astype(jnp.bfloat16), grad_t_ref[h, at, :], preferred_element_type=jnp.float32
                )
                grad_key_ref[h, keys_at, :] += jnp.dot(
                    grad_scores, query_ref[h, at, :], preferred_element_type=jnp.float32
                )
                fresh.append(
                    state[h] + jnp.dot(packed_ref[1, h, :, keys_at], grad_scores, preferred_element_type=jnp.float32)
                )
            return tuple(fresh)

        state = lax.fori_loop(
            range_ref[tile], range_ref[tiles + tile], key_step,
            tuple(jnp.zeros((HEAD_DIM, rows), jnp.float32) for _ in range(heads)),
        )
        for h in range(heads):
            out_ref[0, h, :, at] = (state[h] * scale).astype(jnp.bfloat16)
        return carry

    lax.fori_loop(0, tiles, query_step, 0)
    for h in range(heads):
        out_ref[1, h] = (grad_key_ref[h] * scale).T.astype(jnp.bfloat16)
        out_ref[2, h] = grad_value_ref[h].T.astype(jnp.bfloat16)

def attend_tables(segment_ids):
    length = segment_ids.shape[0]
    rows = math.gcd(length, TILE_ROWS)
    ranges = key_ranges(segment_ids, rows, math.gcd(length, TILE_KEYS))
    return ranges, segment_ids[None], jnp.broadcast_to(segment_ids[:, None], (length, rows))


def attend(packed, ranges, seg_row, seg_col):
    _, heads, _, length = packed.shape
    rows, block, group = seg_col.shape[1], math.gcd(length, TILE_KEYS), math.gcd(heads, TILE_HEADS)
    if length % (2 * block) == 0:
        tiles = length // rows
        block, ranges = 2 * block, jnp.concatenate([ranges[:tiles] // 2, (ranges[tiles:] + 1) // 2])
    area = heads * length * length
    return pl.pallas_call(
        functools.partial(attend_kernel, rows, block),
        grid_spec=pltpu.PrefetchScalarGridSpec(
            num_scalar_prefetch=1,
            grid=(heads // group,),
            in_specs=[
                pl.BlockSpec((1, length), lambda g, r: (0, 0)),
                pl.BlockSpec((length, rows), lambda g, r: (0, 0)),
                pl.BlockSpec((3, group, HEAD_DIM, length), lambda g, r: (0, g, 0, 0)),
            ],
            out_specs=[
                pl.BlockSpec((group, HEAD_DIM, length), lambda g, r: (g, 0, 0)),
                pl.BlockSpec((1, group, length), lambda g, r: (g, 0, 0)),
            ],
            scratch_shapes=[
                pltpu.VMEM((group, length, HEAD_DIM), jnp.bfloat16),
                pltpu.VMEM((group, length, rows), jnp.float32),
            ],
        ),
        out_shape=[
            jax.ShapeDtypeStruct((heads, HEAD_DIM, length), jnp.bfloat16),
            jax.ShapeDtypeStruct((heads // group, group, length), jnp.float32),
        ],
        cost_estimate=pl.CostEstimate(flops=4 * area * 128, transcendentals=area, bytes_accessed=8 * heads * HEAD_DIM * length),
        name="attend",
    )(ranges, seg_row, seg_col, packed)

def attend_back(packed, mixed, grad, totals, ranges, seg_row, seg_col):
    _, heads, _, length = packed.shape
    rows, block, group = seg_col.shape[1], math.gcd(length, TILE_KEYS), math.gcd(heads, TILE_HEADS)
    area = heads * length * length
    return pl.pallas_call(
        functools.partial(attend_back_kernel, rows, block),
        grid_spec=pltpu.PrefetchScalarGridSpec(
            num_scalar_prefetch=1,
            grid=(heads // group,),
            in_specs=[
                pl.BlockSpec((1, length), lambda g, r: (0, 0)),
                pl.BlockSpec((length, rows), lambda g, r: (0, 0)),
                pl.BlockSpec((3, group, HEAD_DIM, length), lambda g, r: (0, g, 0, 0)),
                pl.BlockSpec((group, HEAD_DIM, length), lambda g, r: (g, 0, 0)),
                pl.BlockSpec((group, HEAD_DIM, length), lambda g, r: (g, 0, 0)),
                pl.BlockSpec((1, group, length), lambda g, r: (g, 0, 0)),
            ],
            out_specs=pl.BlockSpec((3, group, HEAD_DIM, length), lambda g, r: (0, g, 0, 0)),
            scratch_shapes=[pltpu.VMEM((group, length, HEAD_DIM), jnp.bfloat16)] * 4
            + [pltpu.VMEM((group, length, HEAD_DIM), jnp.float32)] * 2,
        ),
        out_shape=jax.ShapeDtypeStruct(packed.shape, jnp.bfloat16),
        cost_estimate=pl.CostEstimate(flops=10 * area * 128, transcendentals=area, bytes_accessed=16 * heads * HEAD_DIM * length),
        name="attend_back",
    )(ranges, seg_row, seg_col, packed, mixed, grad, totals)


def split_layer(
    layer_input,
    skip_input,
    segments,
    skip_weight,
    skip_bias,
    attn_norm_gain,
    attn_norm_bias,
    qkv_weight,
    proj_weight,
    proj_bias,
    mlp_norm_gain,
    mlp_norm_bias,
    up_weight,
    up_bias,
    down_weight,
    down_bias,
    cotangent,
):
    micro, length, part_width = layer_input.shape
    width = skip_bias.shape[0]
    hidden_part = up_bias.shape[0]
    model_count = lax.axis_size("mp")
    data_count = lax.axis_size("dp")
    head_count = part_width // HEAD_DIM
    qkv_local = qkv_weight.reshape(width, 3 * part_width)
    grad_skip = jnp.zeros((2, part_width, width), jnp.float32)
    grad_qkv = jnp.zeros((width, 3 * part_width), jnp.float32)
    grad_proj = jnp.zeros((part_width, width), jnp.float32)
    vector_totals = jnp.zeros((7, width), jnp.float32)
    grad_up = jnp.zeros((width, hidden_part), jnp.float32)
    grad_down = jnp.zeros((hidden_part, width), jnp.float32)
    grad_up_bias = jnp.zeros((hidden_part,), jnp.float32)
    results = []
    input_grads = []
    skip_grads = []
    for micro_step in range(micro):
        local_input = layer_input[micro_step]
        local_skip = skip_input[micro_step]
        segment_ids = segments[micro_step]
        grad_output = cotangent[micro_step]
        grad_float = grad_output.astype(jnp.float32)
        base = (
            lax.psum_scatter(
                jnp.dot(local_input, skip_weight[0], preferred_element_type=jnp.float32)
                + jnp.dot(local_skip, skip_weight[1], preferred_element_type=jnp.float32),
                "mp",
                scatter_dimension=0,
                tiled=True,
            )
            + skip_bias
        )
        first_out, first_scaled, first_inverse = normalize(base, attn_norm_gain, attn_norm_bias)
        first_full = lax.all_gather(first_out.astype(jnp.bfloat16), "mp", axis=0, tiled=True)
        tables = attend_tables(segment_ids)
        packed = (
            lax.dot_general(
                qkv_local, first_full, (((0,), (1,)), ((), ())), preferred_element_type=jnp.float32
            )
            .astype(jnp.bfloat16)
            .reshape(3, head_count, HEAD_DIM, length)
        )
        mixed, log_totals = attend(packed, *tables)
        mixture = mixed.reshape(part_width, length).T
        middle = base + (
            lax.psum_scatter(
                jnp.dot(mixture, proj_weight, preferred_element_type=jnp.float32).astype(
                    jnp.bfloat16
                ),
                "mp",
                scatter_dimension=0,
                tiled=True,
            ).astype(jnp.float32)
            + proj_bias
        )
        second_out, second_scaled, second_inverse = normalize(middle, mlp_norm_gain, mlp_norm_bias)
        second_low = second_out.astype(jnp.bfloat16)
        second_full = lax.all_gather(second_low, "mp", axis=0, tiled=True)
        before = jnp.dot(second_full, up_weight, preferred_element_type=jnp.float32) + up_bias
        hidden = jax.nn.gelu(before, approximate=False).astype(jnp.bfloat16)
        result = middle + (
            lax.psum_scatter(
                jnp.dot(hidden, down_weight, preferred_element_type=jnp.float32).astype(
                    jnp.bfloat16
                ),
                "mp",
                scatter_dimension=0,
                tiled=True,
            ).astype(jnp.float32)
            + down_bias
        )
        grad_full = lax.all_gather(grad_output, "mp", axis=0, tiled=True)
        grad_hidden = transposed_right(grad_full, down_weight)
        grad_before = (grad_hidden * gelu_slope(before)).astype(jnp.bfloat16)
        grad_down = grad_down + transposed_left(hidden, grad_full)
        grad_up = grad_up + transposed_left(second_full, grad_before)
        grad_up_bias = grad_up_bias + jnp.sum(grad_before.astype(jnp.float32), axis=0)
        grad_second = lax.psum_scatter(
            transposed_right(grad_before, up_weight).astype(jnp.bfloat16),
            "mp",
            scatter_dimension=0,
            tiled=True,
        ).astype(jnp.float32)
        results.append(result.astype(jnp.bfloat16))
        grad_middle = grad_float + normalize_back(
            grad_second, second_scaled, second_inverse, mlp_norm_gain
        )
        grad_branch = grad_middle.astype(jnp.bfloat16)
        grad_attn_full = lax.all_gather(grad_branch, "mp", axis=0, tiled=True)
        grad_proj = grad_proj + transposed_left(mixture, grad_attn_full)
        grad_mixture = transposed_right(proj_weight, grad_attn_full).astype(jnp.bfloat16)
        grad_packed = attend_back(
            packed, mixed, grad_mixture.reshape(head_count, HEAD_DIM, length), log_totals, *tables
        )
        grad_projected = grad_packed.reshape(3 * part_width, length).T
        grad_qkv = grad_qkv + transposed_left(first_full, grad_projected)
        grad_first = lax.psum_scatter(
            transposed_right(grad_projected, qkv_local).astype(jnp.bfloat16),
            "mp",
            scatter_dimension=0,
            tiled=True,
        ).astype(jnp.float32)
        grad_base = grad_middle + normalize_back(
            grad_first, first_scaled, first_inverse, attn_norm_gain
        )
        grad_base_low = grad_base.astype(jnp.bfloat16)
        grad_base_full = lax.all_gather(grad_base_low, "mp", axis=0, tiled=True)
        grad_skip = grad_skip + jnp.stack(
            [
                transposed_left(local_input, grad_base_full),
                transposed_left(local_skip, grad_base_full),
            ]
        )
        input_grads.append(transposed_right(grad_base_full, skip_weight[0]).astype(jnp.bfloat16))
        skip_grads.append(transposed_right(grad_base_full, skip_weight[1]).astype(jnp.bfloat16))
        vector_totals = vector_totals + jnp.stack(
            [
                jnp.sum(grad_base_low.astype(jnp.float32), axis=0),
                jnp.sum(grad_first * first_scaled, axis=0),
                jnp.sum(grad_first, axis=0),
                jnp.sum(grad_branch.astype(jnp.float32), axis=0),
                jnp.sum(grad_second * second_scaled, axis=0),
                jnp.sum(grad_second, axis=0),
                jnp.sum(grad_float, axis=0),
            ]
        )
    grad_scale = (micro * length * data_count) ** (-0.5)
    up_bias_vector = lax.dynamic_update_slice(
        jnp.zeros((hidden_part * model_count,), jnp.float32),
        grad_up_bias,
        (lax.axis_index("mp") * hidden_part,),
    )
    vector_sums, up_bias_sum = lax.psum((vector_totals, up_bias_vector), ("dp", "mp"))
    skip_share, qkv_share, proj_share, up_share, down_share = (
        lax.psum_scatter(
            grad_skip.astype(jnp.bfloat16), "dp", scatter_dimension=2, tiled=True
        ).astype(jnp.float32),
        lax.psum_scatter(
            grad_qkv.reshape(width, 3, part_width).astype(jnp.bfloat16),
            "dp",
            scatter_dimension=0,
            tiled=True,
        ).astype(jnp.float32),
        lax.psum_scatter(
            grad_proj.astype(jnp.bfloat16), "dp", scatter_dimension=1, tiled=True
        ).astype(jnp.float32),
        lax.psum_scatter(
            grad_up.astype(jnp.bfloat16), "dp", scatter_dimension=0, tiled=True
        ).astype(jnp.float32),
        lax.psum_scatter(
            grad_down.astype(jnp.bfloat16), "dp", scatter_dimension=1, tiled=True
        ).astype(jnp.float32),
    )
    return (
        jnp.stack(results),
        jnp.stack(input_grads),
        jnp.stack(skip_grads),
        skip_share * grad_scale,
        vector_sums[0] * grad_scale,
        vector_sums[1] * grad_scale,
        vector_sums[2] * grad_scale,
        qkv_share * grad_scale,
        proj_share * grad_scale,
        vector_sums[3] * grad_scale,
        vector_sums[4] * grad_scale,
        vector_sums[5] * grad_scale,
        up_share * grad_scale,
        up_bias_sum * grad_scale,
        down_share * grad_scale,
        vector_sums[6] * grad_scale,
    )


def swap_axis(value):
    return lax.ppermute(value, "mp", [(0, 1), (1, 0)])


def swap_bit(value, bit):
    count = lax.axis_size("dp")
    return lax.ppermute(value, "dp", [(index, index ^ bit) for index in range(count)])


def pick(value, index, axis=0):
    return lax.dynamic_index_in_dim(value, index, axis, keepdims=False)


def fetch_half(weight, place):
    rows = weight.shape[0] // 4
    at = place & 3
    near = swap_axis(lax.dynamic_slice_in_dim(weight, at * rows, rows))
    side = swap_bit(near, 2)
    whole = jnp.zeros_like(weight)
    pieces = ((near, at), (side, at ^ 2), (swap_bit(near, 1), at ^ 1), (swap_bit(side, 1), at ^ 3))
    for piece, slot in pieces:
        whole = lax.dynamic_update_slice_in_dim(whole, piece, slot * rows, 0)
    return whole


def add_low(left, right):
    return (left.astype(jnp.float32) + right.astype(jnp.float32)).astype(jnp.bfloat16)


def tie(*values):
    return lax.optimization_barrier(values)


def after(value, *earlier):
    return lax.optimization_barrier((value, *earlier))[0]


class Share:
    def __init__(self, place, *arrays):
        self.place, self.bits = place, [8, 4, 2, 1]
        self.values = [v.reshape(2, 2, 2, 2, v.shape[0] // 16, v.shape[1]) for v in arrays]

    def halve(self, bit):
        axis, mine = self.bits.index(bit), (self.place // bit) & 1
        moved = [swap_bit(pick(v, 1 - mine, axis), bit) for v in self.values]
        self.values = [add_low(pick(v, mine, axis), w) for v, w in zip(self.values, moved)]
        self.bits.remove(bit)

    def cross(self):
        own, other = self.values
        self.values = [add_low(own, swap_axis(other))]


def hold(main, *shares):
    flat = tie(main, *(v for share in shares for v in share.values))
    at = 1
    for share in shares:
        share.values = list(flat[at : at + len(share.values)])
        at += len(share.values)
    return flat[0]


def whole_layer(
    layer_input,
    skip_input,
    segments,
    skip_weight,
    skip_bias,
    attn_norm_gain,
    attn_norm_bias,
    qkv_weight,
    proj_weight,
    proj_bias,
    mlp_norm_gain,
    mlp_norm_bias,
    up_weight,
    up_bias,
    down_weight,
    down_bias,
    cotangent,
):
    micro, length, part = layer_input.shape
    width = skip_bias.shape[0]
    hidden_part = up_bias.shape[0]
    heads = part // HEAD_DIM
    rows_half = length // 2
    low = jnp.bfloat16
    mine = lax.axis_index("mp")
    place = lax.axis_index("dp")
    first_half = mine == 0

    def ordered(own, other, axis):
        return jnp.where(
            first_half, jnp.concatenate([own, other], axis), jnp.concatenate([other, own], axis)
        )

    def dot(left, right):
        return jnp.dot(left, right, preferred_element_type=jnp.float32)

    def bend(before):
        phi = 0.5 * (1.0 + lax.erf(before * 0.7071067811865476))
        bell = jnp.exp(-0.5 * before * before) * 0.3989422804014327
        return (before * phi).astype(low), (phi + before * bell).astype(low)

    with_other = swap_axis(pick(layer_input, 1 - mine))
    with_skip = swap_axis(pick(skip_input, 1 - mine))
    skip_own = skip_weight.reshape(2 * part, width)
    skip_other = fetch_half(skip_own, place)
    own_input, own_skip = pick(layer_input, mine), pick(skip_input, mine)
    base = dot(own_input, skip_weight[0]) + dot(own_skip, skip_weight[1]) + skip_bias
    qkv_own = qkv_weight.reshape(width, 3 * part)
    qkv_other = fetch_half(after(qkv_own, base), place)
    proj_other = fetch_half(after(proj_weight, base), place)
    base = base + dot(with_other, skip_other[:part]) + dot(with_skip, skip_other[part:])
    up_late, down_late, bias_late, cotangent_late, base = tie(
        up_weight, down_weight, up_bias, pick(cotangent, 1 - mine), base
    )
    up_other = fetch_half(up_late, place)
    up_bias_other = swap_axis(bias_late)
    down_other = fetch_half(down_late, place)
    grad_other = swap_axis(cotangent_late)
    segment_ids = pick(segments, mine)
    tables = attend_tables(segment_ids)

    first_out, first_scaled, first_inverse = normalize(base, attn_norm_gain, attn_norm_bias)
    first = first_out.astype(low)
    middle = base
    saved = []
    for weight, proj in ((qkv_own, proj_weight), (qkv_other, proj_other)):
        packed = (
            lax.dot_general(weight, first, (((0,), (1,)), ((), ())), preferred_element_type=jnp.float32)
            .astype(low)
            .reshape(3, heads, HEAD_DIM, length)
        )
        mixed, totals = attend(packed, *tables)
        saved.append((packed, mixed, totals))
        middle = middle + transposed_left(mixed.reshape(part, length), proj)
    middle = middle + proj_bias
    second_out, second_scaled, second_inverse = normalize(middle, mlp_norm_gain, mlp_norm_bias)
    second = second_out.astype(low)
    grad_out = ordered(pick(cotangent, mine), grad_other, 0)
    result = middle
    hidden, slope, down_grads = [], [], []
    for up, bias, down in ((up_weight, up_bias, down_weight), (up_other, up_bias_other, down_other)):
        act, bent = bend(dot(second, up) + bias)
        hidden.append(act)
        slope.append(bent)
        result = result + dot(act, down)
        down_grads.append(transposed_left(grad_out, act).astype(low))
    result = (result + down_bias).astype(low)
    down_share = Share(place, *down_grads)
    result = hold(result, down_share).reshape(2, rows_half, width)
    layer_output = ordered(pick(result, mine)[None], swap_axis(pick(result, 1 - mine))[None], 0)

    down_share.halve(1)
    up_grads, up_bias_grads, before_grads = [], [], []
    for step in range(2):
        down, bent = ((down_weight, slope[0]), (down_other, slope[1]))[step]
        grad_before = (transposed_right(grad_out, down) * bent.astype(jnp.float32)).astype(low)
        if step == 0:
            grad_before = hold(grad_before, down_share)
            down_share.halve(2)
        before_grads.append(grad_before)
        up_grads.append(transposed_left(second, grad_before).astype(low))
        up_bias_grads.append(jnp.sum(grad_before.astype(jnp.float32), axis=0))
    up_share = Share(place, *up_grads)
    before_grads[1] = hold(before_grads[1], up_share)
    up_share.halve(1)
    grad_second = transposed_right(before_grads[0], up_weight) + transposed_right(before_grads[1], up_other)
    grad_second = hold(grad_second, up_share)
    up_share.halve(4)

    grad_float = grad_out.astype(jnp.float32)
    grad_middle = grad_float + normalize_back(grad_second, second_scaled, second_inverse, mlp_norm_gain)
    grad_branch = grad_middle.astype(low)
    vectors = [
        jnp.sum(grad_branch.astype(jnp.float32), axis=0),
        jnp.sum(grad_second * second_scaled, axis=0),
        jnp.sum(grad_second, axis=0),
        jnp.sum(grad_float, axis=0),
        ordered(*up_bias_grads, 0),
    ]

    def proj_back(mixed):
        return lax.dot_general(
            grad_branch,
            mixed.reshape(part, length),
            (((0,), (1,)), ((), ())),
            preferred_element_type=jnp.float32,
        ).astype(low)

    def mixture_back(proj):
        return transposed_right(proj, grad_branch).astype(low).reshape(heads, HEAD_DIM, length)

    def qkv_back(grad_packed):
        return lax.dot_general(
            first, grad_packed, (((0,), (1,)), ((), ())), preferred_element_type=jnp.float32
        ).astype(low)

    def first_back(grad_packed, weight):
        return lax.dot_general(
            grad_packed, weight, (((0,), (1,)), ((), ())), preferred_element_type=jnp.float32
        )

    proj_share = Share(place, proj_back(saved[0][1]), proj_back(saved[1][1]))
    grad_mixture = mixture_back(proj_other)
    grad_mixture_own = mixture_back(proj_weight)
    grad_mixture = hold(grad_mixture, down_share, proj_share)
    down_share.cross()
    proj_share.halve(1)
    packed, mixed, totals = saved[1]
    grad_packed = attend_back(packed, mixed, grad_mixture, totals, *tables)
    grad_packed = hold(grad_packed, down_share, up_share, proj_share).reshape(3 * part, length)
    down_share.halve(4)
    up_share.halve(2)
    proj_share.halve(4)
    other_share = Share(place, qkv_back(grad_packed))
    grad_first = first_back(grad_packed, qkv_other)
    grad_mixture_own = hold(grad_mixture_own, other_share)
    other_share.halve(1)
    packed, mixed, totals = saved[0]
    grad_packed = attend_back(packed, mixed, grad_mixture_own, totals, *tables)
    grad_packed = hold(grad_packed, down_share, up_share, proj_share, other_share).reshape(3 * part, length)
    other_share.halve(2)
    up_share.cross()
    down_share.halve(8)
    proj_share.halve(2)

    grad_first = grad_first + first_back(grad_packed, qkv_own)
    grad_base = (
        grad_middle + normalize_back(grad_first, first_scaled, first_inverse, attn_norm_gain)
    ).astype(low)

    def input_back(weight):
        return transposed_right(grad_base, weight).astype(low)[None]

    sent = [swap_axis(input_back(skip_other[side * part : (side + 1) * part])) for side in range(2)]
    grad_packed_late = after(grad_packed, grad_base)
    own_share = Share(place, qkv_back(grad_packed_late))
    own_share.halve(1)
    skip_low = transposed_left(grad_base, jnp.concatenate([own_input, own_skip], axis=1)).astype(low)
    skip_low = hold(skip_low, own_share, other_share, up_share, proj_share)
    own_share.halve(2)
    other_share.halve(4)
    up_share.halve(8)
    proj_share.halve(8)
    skip_share = Share(place, skip_low)
    skip_share.halve(1)
    skip_away = Share(
        place, transposed_left(grad_base, jnp.concatenate([with_other, with_skip], axis=1)).astype(low)
    )
    skip_away.halve(1)
    vectors += [
        jnp.sum(grad_base.astype(jnp.float32), axis=0),
        jnp.sum(grad_first * first_scaled, axis=0),
        jnp.sum(grad_first, axis=0),
    ]
    vector = jnp.concatenate(vectors)
    vector = vector + swap_bit(vector, 1)
    vector = hold(vector, skip_share, skip_away, own_share, other_share, up_share, proj_share)
    vector = vector + swap_bit(vector, 4)
    skip_share.halve(4)
    skip_away.halve(2)
    own_share.halve(4)
    other_share.halve(8)
    proj_share.cross()
    vector = hold(vector, skip_share, skip_away, own_share, other_share, proj_share)
    vector = vector + swap_bit(vector, 2)
    skip_share.halve(2)
    skip_away.halve(4)
    own_share.halve(8)
    vector = hold(vector, skip_share, skip_away, own_share)
    vector = vector + swap_bit(vector, 8)
    skip_share.halve(8)
    skip_away.halve(8)
    vector = hold(vector, skip_share, skip_away)
    vector = vector + swap_axis(vector)
    skip_share.values += skip_away.values
    skip_share.cross()
    qkv_share = Share(place)
    qkv_share.values = own_share.values + other_share.values
    qkv_share.cross()
    kept = tie(*(input_back(skip_weight[side]) for side in range(2)), *skip_share.values)
    input_grad, skip_grad = (ordered(kept[side], sent[side], 0) for side in range(2))
    skip_share, qkv_share, proj_share, up_share, down_share = (
        share.values[0].astype(jnp.float32) for share in (skip_share, qkv_share, proj_share, up_share, down_share)
    )
    grad_scale = (micro * length * lax.axis_size("dp")) ** (-0.5)
    vector = vector * grad_scale
    hidden_width = 2 * hidden_part
    vectors = vector[: 4 * width].reshape(4, width)
    late = vector[4 * width + hidden_width :].reshape(3, width)
    return (
        layer_output,
        input_grad,
        skip_grad,
        skip_share.T.reshape(2, part, -1) * grad_scale,
        late[0],
        late[1],
        late[2],
        qkv_share.reshape(-1, 3, part) * grad_scale,
        proj_share.T * grad_scale,
        vectors[0],
        vectors[1],
        vectors[2],
        up_share * grad_scale,
        vector[4 * width : 4 * width + hidden_width],
        down_share.T * grad_scale,
        vectors[3],
    )


def body(*arrays):
    micro, _, part = arrays[0].shape
    if lax.axis_size("mp") == micro == 2 and lax.axis_size("dp") == 16:
        return whole_layer(*arrays)
    return split_layer(*arrays)


def solution(mesh):
    return jax.shard_map(
        body,
        mesh=mesh,
        in_specs=(
            P(None, "dp", "mp"),
            P(None, "dp", "mp"),
            P(None, "dp"),
            P(None, "mp", None),
            P(),
            P(),
            P(),
            P(None, None, "mp"),
            P("mp", None),
            P(),
            P(),
            P(),
            P(None, "mp"),
            P("mp"),
            P("mp", None),
            P(),
            P(None, ("dp", "mp"), None),
        ),
        out_specs=(
            P(None, ("dp", "mp"), None),
            P(None, "dp", "mp"),
            P(None, "dp", "mp"),
            P(None, "mp", "dp"),
            P(),
            P(),
            P(),
            P("dp", None, "mp"),
            P("mp", "dp"),
            P(),
            P(),
            P(),
            P("dp", "mp"),
            P(),
            P("mp", "dp"),
            P(),
        ),
        check_vma=False,
    )
```
